32 devices in a mesh: tm: 4 (over x, core), pair: 8 (over z, y).
Axes of the slice: x: 2, y: 2, z: 4, core: 2. Of those that a mesh axis runs over, the one named last changes fastest.
Arguments:
- orbitals: bfloat16 [8192, 512], P('pair', 'tm'), may hold values from -1.5 to 1.5
- level_gap: float32 [512], replicated, may hold values from 0.05 to 1.5
- screened: bfloat16 [8, 32, 1024, 1024], P('tm', 'pair'), may hold values from -0.008972168 to 0.008972168
- pair_blocks: int32 [32, 2], P('pair'), may hold values from 0 to 7, as said below
Outputs:
- self_energy: float32 [8, 512, 512], P('tm', 'pair')
The draws below stay inside these ranges and needn't reach their ends.
Inputs may be any that keep to these rules, and one draw needn't show every extreme that they name: `pair_blocks`: each row names two point blocks a <= c; no unordered pair appears in two rows; the pair (0, 7) appears in every draw.
All inputs are finite; a program needn't handle non-finite values.
Results may differ from the reference program's by a relative error of at most 0.0049.
Values may be sent and summed in bfloat16 or wider, within the bound.
A program may use at most 128 MiB of HBM per device.

```python
import math
import jax
import jax.numpy as jnp
from jax import lax

NORB = 512
NOCC = 128
BLK = 1024
NT = 8
PAIRS = 32
NPTS = 8192
N_PAIR = 8


def draw_pair_blocks(key, part):
    count = N_PAIR * N_PAIR
    flat = jnp.arange(count, dtype=jnp.int32)
    first = flat // N_PAIR
    second = flat % N_PAIR
    ranks = jax.random.permutation(jax.random.fold_in(key, 11), count).astype(jnp.int32)
    ranks = jnp.where(first <= second, ranks, ranks + count)
    ranks = jnp.where((first == 0) & (second == N_PAIR - 1), jnp.int32(-1), ranks)
    order = jnp.argsort(ranks, stable=True)[:PAIRS]
    shuffle = jax.random.permutation(jax.random.fold_in(key, 23), PAIRS)
    picked = order[shuffle]
    return jnp.stack([first[picked], second[picked]], axis=1).astype(jnp.int32)


def block_levels(own_key, extent, split, least, largest):
    def one(dim, shards_of):
        steps = jax.random.uniform(jax.random.fold_in(jax.random.fold_in(own_key, 6), dim), (shards_of,), jnp.float32, least / len(split), largest / len(split))
        return jnp.repeat(jnp.exp(steps), extent[dim] // shards_of).reshape((-1,) + (1,) * (len(extent) - dim - 1))

    level = one(*split[0])
    for cut in split[1:]:
        level = level * one(*cut)
    return level


def scatter_about(stream_key, extent, scale, limit, pieces=(), held_as=jnp.bfloat16):
    entries = scale * jax.random.normal(stream_key, extent, jnp.float32)
    if pieces:
        entries = entries * block_levels(stream_key, extent, pieces, -0.22, 0.18)
    return jnp.clip(entries, -limit, limit).astype(held_as)


def setup_inputs(seed: int = 0) -> dict:
    keys = jax.random.split(jax.random.key(seed), 5)
    return {
        "orbitals": scatter_about(keys[0], (NPTS, NORB), 0.25, 1.5, ((0, 8), (1, 4))),
        "level_gap": jnp.clip(jnp.exp(jax.random.uniform(keys[1], (NORB,), jnp.float32, math.log(0.05), math.log(1.5))), 0.05, 1.5),
        "screened": scatter_about(keys[2], (NT, PAIRS, BLK, BLK), 0.0015, 0.008972168, ((0, 4), (1, 8))),
        "pair_blocks": draw_pair_blocks(jax.random.fold_in(keys[4], 71), 0),
    }


def reference(orbitals, level_gap, screened, pair_blocks):
    blocks = orbitals.reshape(NPTS // BLK, BLK, NORB)
    tau = 6.0 * (jnp.arange(NT, dtype=jnp.float32) + 0.5) / NT
    signs = jnp.where(jnp.arange(NORB) < NOCC, 1.0, -1.0).astype(jnp.float32)
    factors = signs[None, :] * jnp.exp(-level_gap[None, :] * tau[:, None])

    def per_time(items):
        factor, tiles = items

        def step(total, item):
            tile, pair = item
            left = blocks[pair[0]]
            right = blocks[pair[1]]
            scaled = (left.astype(jnp.float32) * factor[None, :]).astype(jnp.bfloat16)
            green = lax.dot_general(scaled, right, (((1,), (1,)), ((), ())), preferred_element_type=jnp.float32)
            product = (green * tile.astype(jnp.float32)).astype(jnp.bfloat16)
            half = lax.dot_general(left, product, (((0,), (0,)), ((), ())), preferred_element_type=jnp.float32).astype(jnp.bfloat16)
            block = jnp.dot(half, right, preferred_element_type=jnp.float32)
            weight = jnp.where(pair[0] == pair[1], 0.5, 1.0).astype(jnp.float32)
            return total + weight * (block + block.T), None

        total, unused = lax.scan(step, jnp.zeros((NORB, NORB), jnp.float32), (tiles, pair_blocks))
        return total

    return lax.map(per_time, (factors, screened))
```

```python
import functools

import jax
import jax.numpy as jnp
from jax import lax
from jax.experimental import pallas as pl
from jax.experimental.pallas import tpu as pltpu
from jax.sharding import PartitionSpec as P

NOCC = 128
MESH = pl.DeviceIdType.MESH
ROWS = 512


def kernel(
    tm_size, pair_size, pb, gap, orb_in, scr_in, out,
    orb, scr, lt, u, acc, part, rbuf,
    own_sem, scr_sem, ssem, rsem, xs_sem, xr_sem,
):
    times, pairs = scr.shape[0], scr.shape[1]
    points, cols = orb_in.shape
    norb = orb.shape[2]
    half = points // 2
    line = pair_size // 2
    tm = lax.axis_index("tm")
    me = lax.axis_index("pair")
    h, c = tm // 2, tm % 2
    z, y = me // 2, me % 2
    tm_x = (1 - h) * 2 + c
    tm_p = h * 2 + (1 - c)
    me_y = z * 2 + (1 - y)

    barrier = pltpu.get_barrier_semaphore()
    pl.semaphore_signal(barrier, inc=1, device_id=(tm_x, me), device_id_type=MESH)
    pl.semaphore_signal(barrier, inc=1, device_id=(tm_p, me), device_id_type=MESH)
    for k in range(1, pair_size):
        pl.semaphore_signal(
            barrier, inc=1, device_id=(tm, (me + k) % pair_size), device_id_type=MESH
        )

    own_col = pl.ds(pl.multiple_of(tm * cols, cols), cols)
    own = pltpu.make_async_copy(orb_in, orb.at[me, :, own_col], own_sem.at[0])
    own.start()
    pl.semaphore_wait(barrier, pair_size + 1)

    def region(block, column, first=0, count=points):
        return orb.at[
            block, pl.ds(first, count), pl.ds(pl.multiple_of(column * cols, cols), cols)
        ]

    def copy(src, dst, sk, rk, z0, dev):
        return pltpu.make_async_remote_copy(
            src_ref=src, dst_ref=dst, send_sem=ssem.at[sk, z0], recv_sem=rsem.at[rk, z0],
            device_id=dev, device_id_type=MESH,
        )

    def main(z0):
        return region(z0 * 2 + y, tm)

    def c_up(z0, src=None):
        return copy(main(z0) if src is None else src, main(z0), 0, 0, z0, (tm, me + 2))

    def c_down(z0, src=None):
        return copy(main(z0) if src is None else src, main(z0), 1, 0, z0, (tm, me - 2))

    def c_x(z0, src=None):
        return copy(main(z0) if src is None else src, main(z0), 2, 1, z0, (tm_x, me))

    def c_y(z0, src=None):
        return copy(main(z0) if src is None else src, main(z0), 3, 2, z0, (tm, me_y))

    def c_p(z0, src=None):
        return copy(main(z0) if src is None else src, main(z0), 4, 5, z0, (tm_p, me))

    def from_x(z0, *rows):
        return region(z0 * 2 + y, tm_x, *rows)

    def from_y(z0, *rows):
        return region(z0 * 2 + 1 - y, tm, *rows)

    def from_d(z0, *rows):
        return region(z0 * 2 + 1 - y, tm_x, *rows)

    def c_px(z0):
        return copy(from_x(z0), from_x(z0), 5, 6, z0, (tm_p, me))

    def c_py(z0):
        return copy(from_y(z0), from_y(z0), 6, 7, z0, (tm_p, me))

    def c_pd(z0):
        return copy(from_d(z0), from_d(z0), 7, 8, z0, (tm_p, me))

    def c_xy(z0):
        return copy(from_x(z0, 0, half), from_x(z0, 0, half), 8, 3, z0, (tm, me_y))

    def c_yx(z0):
        return copy(from_y(z0, half, half), from_y(z0, half, half), 9, 4, z0, (tm_x, me))

    def arrived(dst, rk, z0):
        copy(dst, dst, 0, rk, z0, (tm_p, me)).wait_recv()

    def guard(cond, f):
        if cond is None:
            f()
        else:
            pl.when(cond)(f)

    groups = [(z, None, 0)]
    for d in range(1, line):
        groups.append((z - d, z - d >= 0, 1))
        groups.append((z + d, z + d < line, 2))

    def stage_a(group):
        z0, cond, way = group

        def body():
            src = orb_in if way == 0 else None
            if way:
                arrived(main(z0), 0, z0)
            if way in (0, 1):
                pl.when(z + 1 < line)(lambda: c_up(z0, src).start())
            if way in (0, 2):
                pl.when(z >= 1)(lambda: c_down(z0, src).start())
            c_x(z0, src).start()
            c_y(z0, src).start()
            c_p(z0, src).start()

        guard(cond, body)

    def stage_b(group):
        z0, cond, way = group

        def body():
            arrived(from_x(z0), 1, z0)
            c_xy(z0).start()
            c_px(z0).start()
            arrived(from_y(z0), 2, z0)
            c_yx(z0).start()
            c_py(z0).start()

        guard(cond, body)

    def stage_c(group):
        z0, cond, way = group

        def body():
            arrived(from_d(z0, 0, half), 3, z0)
            arrived(from_d(z0, half, half), 4, z0)
            c_pd(z0).start()

        guard(cond, body)

    def tile_copy(t, p):
        return pltpu.make_async_copy(scr_in.at[t, p], scr.at[t, p], scr_sem.at[t, p])

    stage_a(groups[0])
    for t in range(times):
        for p in range(pairs):
            tile_copy(t, p).start()
    count = len(groups)
    for k in range(1, count + 2):
        if k < count:
            stage_a(groups[k])
        if 0 <= k - 1 < count:
            stage_b(groups[k - 1])
        if 0 <= k - 2 < count:
            stage_c(groups[k - 2])

    own.wait()
    for z0 in range(line):
        arrived(region(z0 * 2 + y, tm_p), 5, z0)
        other = (1 - h) * 2 + (1 - c)
        arrived(region(z0 * 2 + y, other), 6, z0)
        arrived(region(z0 * 2 + 1 - y, tm_p), 7, z0)
        arrived(region(z0 * 2 + 1 - y, other), 8, z0)
    for z0, cond, way in groups:
        def ends(z0=z0, way=way):
            src = orb_in if way == 0 else None
            if way in (0, 1):
                pl.when(z + 1 < line)(lambda: c_up(z0, src).wait_send())
            if way in (0, 2):
                pl.when(z >= 1)(lambda: c_down(z0, src).wait_send())
            for one in (c_x(z0, src), c_y(z0, src), c_p(z0, src)):
                one.wait_send()
            for one in (c_px(z0), c_py(z0), c_pd(z0), c_xy(z0), c_yx(z0)):
                one.wait_send()

        guard(cond, ends)

    share = out.shape[1]

    def share_copy(t, peer, slot):
        return pltpu.make_async_remote_copy(
            src_ref=part.at[t, pl.ds(pl.multiple_of(peer * share, share), share), :],
            dst_ref=rbuf.at[t, slot],
            send_sem=xs_sem.at[t, peer], recv_sem=xr_sem.at[t, slot],
            device_id=(tm, peer), device_id_type=MESH,
        )

    def peers():
        return [(me + k) % pair_size for k in range(1, pair_size)]

    lane = lax.broadcasted_iota(jnp.int32, (1, norb), 1)
    sign = jnp.where(lane < NOCC, 1.0, -1.0).astype(jnp.float32)
    for t in range(times):
        moment = jnp.full((1, norb), tm * times + t, jnp.int32).astype(jnp.float32)
        tau = 6.0 * (moment + 0.5) / (tm_size * times)
        factor = sign * jnp.exp(-gap[...] * tau)
        acc[...] = jnp.zeros_like(acc)

        def pair_step(p, carry):
            a = pb[p, 0]
            b = pb[p, 1]
            scaled_by = factor * jnp.where(a == b, 0.5, 1.0).astype(jnp.float32)
            tile_copy(t, p).wait()
            for r in range(0, points, ROWS):
                left = orb[a, pl.ds(r, ROWS), :]
                scaled = (left.astype(jnp.float32) * scaled_by).astype(jnp.bfloat16)
                green = lax.dot_general(
                    scaled, orb[b], (((1,), (1,)), ((), ())),
                    preferred_element_type=jnp.float32,
                )
                product = (green * scr[t, p, pl.ds(r, ROWS), :].astype(jnp.float32)).astype(
                    jnp.bfloat16
                )
                u[pl.ds(r, ROWS), :] = jnp.dot(
                    product, orb[b], preferred_element_type=jnp.float32
                ).astype(jnp.bfloat16)
                if t == 0:
                    lt[p, :, pl.ds(r, ROWS)] = left.T
            acc[...] += jnp.dot(lt[p], u[...], preferred_element_type=jnp.float32)
            return carry

        lax.fori_loop(0, pairs, pair_step, 0)
        total = acc[...]
        acc[...] = total + total.T
        part[t] = acc[...].astype(jnp.bfloat16)
        for peer in peers():
            share_copy(t, peer, me).start()
        out[t] = acc[pl.ds(pl.multiple_of(me * share, share), share), :]

    for t in range(times):
        for peer in peers():
            share_copy(t, peer, peer).wait_recv()
        total = out[t]
        for peer in peers():
            total = total + rbuf[t, peer].astype(jnp.float32)
        out[t] = total
    for t in range(times):
        for peer in peers():
            share_copy(t, peer, me).wait_send()


def shards(tm_size, pair_size, orbitals, level_gap, screened, pair_blocks):
    points, cols = orbitals.shape
    times, pairs = screened.shape[:2]
    norb = level_gap.shape[0]
    share = norb // pair_size
    line = pair_size // 2
    bf16, f32 = jnp.bfloat16, jnp.float32
    return pl.pallas_call(
        functools.partial(kernel, tm_size, pair_size),
        out_shape=jax.ShapeDtypeStruct((times, share, norb), f32),
        in_specs=[
            pl.BlockSpec(memory_space=pltpu.SMEM),
            pl.BlockSpec(memory_space=pltpu.VMEM),
            pl.BlockSpec(memory_space=pl.ANY),
            pl.BlockSpec(memory_space=pl.ANY),
        ],
        out_specs=pl.BlockSpec(memory_space=pltpu.VMEM),
        scratch_shapes=[
            pltpu.VMEM((pair_size, points, norb), bf16),
            pltpu.VMEM((times, pairs, points, points), bf16),
            pltpu.VMEM((pairs, norb, points), bf16),
            pltpu.VMEM((points, norb), bf16),
            pltpu.VMEM((norb, norb), f32),
            pltpu.VMEM((times, norb, norb), bf16),
            pltpu.VMEM((times, pair_size, share, norb), bf16),
            pltpu.SemaphoreType.DMA((1,)),
            pltpu.SemaphoreType.DMA((times, pairs)),
            pltpu.SemaphoreType.DMA((10, line)),
            pltpu.SemaphoreType.DMA((9, line)),
            pltpu.SemaphoreType.DMA((times, pair_size)),
            pltpu.SemaphoreType.DMA((times, pair_size)),
        ],
        compiler_params=pltpu.CompilerParams(
            collective_id=0, has_side_effects=True, vmem_limit_bytes=63 * 1024 * 1024
        ),
    )(pair_blocks, level_gap.reshape(1, norb), orbitals, screened)


def solution(mesh):
    return jax.shard_map(
        functools.partial(shards, mesh.shape["tm"], mesh.shape["pair"]),
        mesh=mesh,
        in_specs=(P("pair", "tm"), P(), P("tm", "pair", None, None), P("pair", None)),
        out_specs=P("tm", "pair", None),
        check_vma=False,
    )
```

```python
import functools

import jax
import jax.numpy as jnp
from jax import lax
from jax.experimental import pallas as pl
from jax.experimental.pallas import tpu as pltpu
from jax.sharding import PartitionSpec as P

NOCC = 128
MESH = pl.DeviceIdType.MESH
ROWS = 512


def kernel(
    tm_size, pair_size, pb, gap, orb_in, scr_in, out,
    orb, scr, lt, u, acc, part, rbuf, zpart,
    own_sem, scr_sem, ssem, rsem, xs_sem, xr_sem,
):
    times, pairs = scr.shape[0], scr.shape[1]
    points, cols = orb_in.shape
    norb = orb.shape[2]
    half, quarter = points // 2, points // 4
    line = pair_size // 2
    tm = lax.axis_index("tm")
    me = lax.axis_index("pair")
    h, c = tm // 2, tm % 2
    z, y = me // 2, me % 2
    tm_x = (1 - h) * 2 + c
    tm_p = h * 2 + (1 - c)
    me_y = z * 2 + (1 - y)

    barrier = pltpu.get_barrier_semaphore()
    pl.semaphore_signal(barrier, inc=1, device_id=(tm_x, me), device_id_type=MESH)
    pl.semaphore_signal(barrier, inc=1, device_id=(tm_p, me), device_id_type=MESH)
    pl.semaphore_signal(barrier, inc=1, device_id=(tm, me_y), device_id_type=MESH)

    @pl.when(z >= 1)
    def _():
        pl.semaphore_signal(barrier, inc=1, device_id=(tm, me - 2), device_id_type=MESH)

    @pl.when(z + 1 < line)
    def _():
        pl.semaphore_signal(barrier, inc=1, device_id=(tm, me + 2), device_id_type=MESH)

    own_col = pl.ds(pl.multiple_of(tm * cols, cols), cols)
    own = pltpu.make_async_copy(orb_in, orb.at[me, :, own_col], own_sem.at[0])
    own.start()
    along = (z + line - 1) // line + (2 * line - 2 - z) // line
    pl.semaphore_wait(barrier, 3 + along)

    def region(block, column, first=0, count=points):
        return orb.at[
            block, pl.ds(first, count), pl.ds(pl.multiple_of(column * cols, cols), cols)
        ]

    def copy(src, dst, sk, rk, z0, dev):
        return pltpu.make_async_remote_copy(
            src_ref=src, dst_ref=dst, send_sem=ssem.at[sk, z0], recv_sem=rsem.at[rk, z0],
            device_id=dev, device_id_type=MESH,
        )

    def main(z0):
        return region(z0 * 2 + y, tm)

    def c_up(z0, src=None):
        return copy(main(z0) if src is None else src, main(z0), 0, 0, z0, (tm, me + 2))

    def c_down(z0, src=None):
        return copy(main(z0) if src is None else src, main(z0), 1, 0, z0, (tm, me - 2))

    def c_x(z0, src=None):
        return copy(main(z0) if src is None else src, main(z0), 2, 1, z0, (tm_x, me))

    def c_y(z0, src=None):
        return copy(main(z0) if src is None else src, main(z0), 3, 2, z0, (tm, me_y))

    def c_p(z0, src=None):
        return copy(main(z0) if src is None else src, main(z0), 4, 5, z0, (tm_p, me))

    def from_x(z0, *rows):
        return region(z0 * 2 + y, tm_x, *rows)

    def from_y(z0, *rows):
        return region(z0 * 2 + 1 - y, tm, *rows)

    def from_d(z0, *rows):
        return region(z0 * 2 + 1 - y, tm_x, *rows)

    def c_px(z0):
        return copy(from_x(z0), from_x(z0), 5, 6, z0, (tm_p, me))

    def c_py(z0):
        return copy(from_y(z0), from_y(z0), 6, 7, z0, (tm_p, me))

    def c_pd(z0):
        return copy(from_d(z0), from_d(z0), 7, 8, z0, (tm_p, me))

    def rows_xy(way):
        return (0, quarter) if way else (0, half)

    def rows_yx(way):
        return (quarter, quarter) if way else (half, half)

    def c_xy(z0, way):
        rows = from_x(z0, *rows_xy(way))
        return copy(rows, rows, 8, 3, z0, (tm, me_y))

    def c_yx(z0, way):
        rows = from_y(z0, *rows_yx(way))
        return copy(rows, rows, 9, 4, z0, (tm_x, me))

    def c_dup(z0):
        rows = from_d(z0, half, half)
        return copy(rows, rows, 10, 9, z0, (tm, me + 2))

    def c_ddown(z0):
        rows = from_d(z0, half, half)
        return copy(rows, rows, 11, 9, z0, (tm, me - 2))

    def arrived(dst, rk, z0):
        copy(dst, dst, 0, rk, z0, (tm_p, me)).wait_recv()

    def guard(cond, f):
        if cond is None:
            f()
        else:
            pl.when(cond)(f)

    groups = [(z, None, 0)]
    for d in range(1, line):
        groups.append((z - d, z - d >= 0, 1))
        groups.append((z + d, z + d < line, 2))

    def stage_a(group):
        z0, cond, way = group

        def body():
            src = orb_in if way == 0 else None
            if way:
                arrived(main(z0), 0, z0)
            if way in (0, 1):
                pl.when(z + 1 < line)(lambda: c_up(z0, src).start())
            if way in (0, 2):
                pl.when(z >= 1)(lambda: c_down(z0, src).start())
            c_x(z0, src).start()
            c_y(z0, src).start()
            c_p(z0, src).start()

        guard(cond, body)

    def stage_b(group):
        z0, cond, way = group

        def body():
            arrived(from_x(z0), 1, z0)
            c_xy(z0, way).start()
            c_px(z0).start()
            arrived(from_y(z0), 2, z0)
            c_yx(z0, way).start()
            c_py(z0).start()

        guard(cond, body)

    def stage_c(group):
        z0, cond, way = group

        def body():
            arrived(from_d(z0, *rows_xy(way)), 3, z0)
            arrived(from_d(z0, *rows_yx(way)), 4, z0)
            if way == 0:
                pl.when(z + 1 < line)(lambda: c_dup(z0).start())
                pl.when(z >= 1)(lambda: c_ddown(z0).start())
            c_pd(z0).start()

        guard(cond, body)

    def stage_r(group):
        z0, cond, way = group

        def body():
            arrived(from_d(z0, half, half), 9, z0)
            if way == 1:
                pl.when(z + 1 < line)(lambda: c_dup(z0).start())
            else:
                pl.when(z >= 1)(lambda: c_ddown(z0).start())

        guard(cond, body)

    def tile_copy(t, p):
        return pltpu.make_async_copy(scr_in.at[t, p], scr.at[t, p], scr_sem.at[t, p])

    stage_a(groups[0])
    for t in range(times):
        for p in range(pairs):
            tile_copy(t, p).start()
    count = len(groups)
    for k in range(1, count + 3):
        if k < count:
            stage_a(groups[k])
        if k == 1:
            pl.when(z >= 1)(lambda: stage_b(groups[0]))
        if k == 2:
            pl.when(z == 0)(lambda: stage_b(groups[0]))
        if k == 4:
            stage_c(groups[0])
        if 1 <= k - 3 < count:
            stage_r(groups[k - 3])
            stage_b(groups[k - 3])
        if 1 <= k - 6 < count:
            stage_c(groups[k - 6])
    for group in groups[max(1, count - 3):]:
        stage_c(group)

    own.wait()
    for z0 in range(line):
        arrived(region(z0 * 2 + y, tm_p), 5, z0)
        other = (1 - h) * 2 + (1 - c)
        arrived(region(z0 * 2 + y, other), 6, z0)
        arrived(region(z0 * 2 + 1 - y, tm_p), 7, z0)
        arrived(region(z0 * 2 + 1 - y, other), 8, z0)
    for z0, cond, way in groups:
        def ends(z0=z0, way=way):
            src = orb_in if way == 0 else None
            def up():
                c_up(z0, src).wait_send()
                c_dup(z0).wait_send()

            def down():
                c_down(z0, src).wait_send()
                c_ddown(z0).wait_send()

            if way in (0, 1):
                pl.when(z + 1 < line)(up)
            if way in (0, 2):
                pl.when(z >= 1)(down)
            for one in (c_x(z0, src), c_y(z0, src), c_p(z0, src)):
                one.wait_send()
            for one in (c_px(z0), c_py(z0), c_pd(z0), c_xy(z0, way), c_yx(z0, way)):
                one.wait_send()

        guard(cond, ends)

    share = out.shape[1]

    def share_copy(t, peer, slot):
        return pltpu.make_async_remote_copy(
            src_ref=part.at[t, pl.ds(pl.multiple_of(peer * share, share), share), :],
            dst_ref=rbuf.at[t, slot],
            send_sem=xs_sem.at[t, peer], recv_sem=xr_sem.at[t, slot],
            device_id=(tm, peer), device_id_type=MESH,
        )

    def peers():
        return [(me + k) % pair_size for k in range(1, pair_size)]

    def far():
        return [(z + k) % line for k in range(1, line)] + [z]

    def y_copy(z1):
        peer = z1 * 2 + 1 - y
        return pltpu.make_async_remote_copy(
            src_ref=part.at[times - 1, pl.ds(pl.multiple_of(peer * share, share), share), :],
            dst_ref=rbuf.at[times - 1, z1 * 2],
            send_sem=xs_sem.at[times - 1, z1 * 2], recv_sem=xr_sem.at[times - 1, z1 * 2],
            device_id=(tm, me_y), device_id_type=MESH,
        )

    def z_copy(z1, slot):
        return pltpu.make_async_remote_copy(
            src_ref=zpart.at[z1], dst_ref=rbuf.at[times - 1, slot * 2 + 1],
            send_sem=xs_sem.at[times - 1, z1 * 2 + 1],
            recv_sem=xr_sem.at[times - 1, slot * 2 + 1],
            device_id=(tm, z1 * 2 + y), device_id_type=MESH,
        )

    lane = lax.broadcasted_iota(jnp.int32, (1, norb), 1)
    sign = jnp.where(lane < NOCC, 1.0, -1.0).astype(jnp.float32)
    for t in range(times):
        moment = jnp.full((1, norb), tm * times + t, jnp.int32).astype(jnp.float32)
        tau = 6.0 * (moment + 0.5) / (tm_size * times)
        factor = sign * jnp.exp(-gap[...] * tau)
        acc[...] = jnp.zeros_like(acc)

        def pair_step(p, carry):
            a = pb[0, p]
            b = pb[1, p]
            scaled_by = factor * jnp.where(a == b, 0.5, 1.0).astype(jnp.float32)
            tile_copy(t, p).wait()
            for r in range(0, points, ROWS):
                left = orb[a, pl.ds(r, ROWS), :]
                scaled = (left.astype(jnp.float32) * scaled_by).astype(jnp.bfloat16)
                green = lax.dot_general(
                    scaled, orb[b], (((1,), (1,)), ((), ())),
                    preferred_element_type=jnp.float32,
                )
                product = (green * scr[t, p, pl.ds(r, ROWS), :].astype(jnp.float32)).astype(
                    jnp.bfloat16
                )
                u[pl.ds(r, ROWS), :] = jnp.dot(
                    product, orb[b], preferred_element_type=jnp.float32
                ).astype(jnp.bfloat16)
                if t == 0:
                    lt[p, :, pl.ds(r, ROWS)] = left.T
            acc[...] += jnp.dot(lt[p], u[...], preferred_element_type=jnp.float32)
            return carry

        lax.fori_loop(0, pairs, pair_step, 0)
        total = acc[...]
        acc[...] = total + total.T
        part[t] = acc[...].astype(jnp.bfloat16)
        if t < times - 1:
            for peer in peers():
                share_copy(t, peer, me).start()
        else:
            for z1 in far():
                y_copy(z1).start()
        out[t] = acc[pl.ds(pl.multiple_of(me * share, share), share), :]

    t = times - 1
    for z1 in far()[:-1]:
        y_copy(z1).wait_recv()
        rows = acc[pl.ds(pl.multiple_of((z1 * 2 + y) * share, share), share), :]
        zpart[z1] = (rows + rbuf[t, z1 * 2].astype(jnp.float32)).astype(jnp.bfloat16)
        z_copy(z1, z).start()
    for t in range(times - 1):
        for peer in peers():
            share_copy(t, peer, peer).wait_recv()
        total = out[t]
        for peer in peers():
            total = total + rbuf[t, peer].astype(jnp.float32)
        out[t] = total
    t = times - 1
    y_copy(z).wait_recv()
    total = out[t] + rbuf[t, z * 2].astype(jnp.float32)
    for z1 in far()[:-1]:
        z_copy(z1, z1).wait_recv()
        total = total + rbuf[t, z1 * 2 + 1].astype(jnp.float32)
    out[t] = total
    for t in range(times - 1):
        for peer in peers():
            share_copy(t, peer, me).wait_send()
    for z1 in far():
        y_copy(z1).wait_send()
    for z1 in far()[:-1]:
        z_copy(z1, z).wait_send()


def shards(tm_size, pair_size, orbitals, level_gap, screened, pair_blocks):
    points, cols = orbitals.shape
    times, pairs = screened.shape[:2]
    norb = level_gap.shape[0]
    share = norb // pair_size
    line = pair_size // 2
    bf16, f32 = jnp.bfloat16, jnp.float32
    return pl.pallas_call(
        functools.partial(kernel, tm_size, pair_size),
        out_shape=jax.ShapeDtypeStruct((times, share, norb), f32),
        in_specs=[
            pl.BlockSpec(memory_space=pltpu.SMEM),
            pl.BlockSpec(memory_space=pltpu.VMEM),
            pl.BlockSpec(memory_space=pl.ANY),
            pl.BlockSpec(memory_space=pl.ANY),
        ],
        out_specs=pl.BlockSpec(memory_space=pltpu.VMEM),
        scratch_shapes=[
            pltpu.VMEM((pair_size, points, norb), bf16),
            pltpu.VMEM((times, pairs, points, points), bf16),
            pltpu.VMEM((pairs, norb, points), bf16),
            pltpu.VMEM((points, norb), bf16),
            pltpu.VMEM((norb, norb), f32),
            pltpu.VMEM((times, norb, norb), bf16),
            pltpu.VMEM((times, pair_size, share, norb), bf16),
            pltpu.VMEM((line, share, norb), bf16),
            pltpu.SemaphoreType.DMA((1,)),
            pltpu.SemaphoreType.DMA((times, pairs)),
            pltpu.SemaphoreType.DMA((12, line)),
            pltpu.SemaphoreType.DMA((10, line)),
            pltpu.SemaphoreType.DMA((times, pair_size)),
            pltpu.SemaphoreType.DMA((times, pair_size)),
        ],
        compiler_params=pltpu.CompilerParams(
            collective_id=0, has_side_effects=True, vmem_limit_bytes=63 * 1024 * 1024
        ),
    )(pair_blocks.T, level_gap.reshape(1, norb), orbitals, screened)


def solution(mesh):
    return jax.shard_map(
        functools.partial(shards, mesh.shape["tm"], mesh.shape["pair"]),
        mesh=mesh,
        in_specs=(P("pair", "tm"), P(), P("tm", "pair", None, None), P("pair", None)),
        out_specs=P("tm", "pair", None),
        check_vma=False,
    )
```
